32 devices in a mesh: grp: 2 (over y), wide: 4 (over z), narrow: 2 (over x), tile: 2 (over core).
Axes of the slice: x: 2, y: 2, z: 4, core: 2. Of those that a mesh axis runs over, the one named last changes fastest.
Arguments:
- green: bfloat16 [32768, 1024], P(('grp', 'wide', 'narrow', 'tile')), parts along dimension 0, may hold values from -0.52734375 to 0.52734375
- log_strength: float32 [32768], P(('grp', 'wide', 'narrow', 'tile')), parts along dimension 0, may hold values from -1 to 1
- observed: float32 [1056, 512], P('grp'), parts along dimension 0, may hold values from -6 to 6
- owner_map: int32 [1056], P('grp'), parts along dimension 0, may hold values from 0 to 527, each once
Outputs:
- new_log_strength: float32 [32768], P(('grp', 'wide', 'narrow', 'tile')), parts along dimension 0
- residual: float32 [1056, 512], P(('grp', 'wide')), parts along dimension 0
The draws below stay inside these ranges and needn't reach their ends.
There are 2 independent parts, one for each index of `grp`. The reference program is written for one: setup_inputs(seed, part) draws one part's arguments, and reference() takes and returns one part's arrays. A program takes and returns all parts, laid end to end along the dimension named above; each array names one. Nothing has to cross between parts.
Inputs may be any that keep to these rules, and one draw needn't show every extreme that they name: `owner_map`: every tile number appears once; the slots form 4 equal runs in order, the k-th run owned by the k-th index of wide.
All inputs are finite; a program needn't handle non-finite values.
Results may differ from the reference program's by a relative error of at most 0.0018.
Values may be sent and summed in bfloat16 or wider, within the bound.
A program may use at most 64 MiB of HBM per device.

```python
import jax
import jax.numpy as jnp
import numpy as np
from jax import lax

NS = 512
NB = 32
STEPS = 2
NPTS = 16384
B = 16
TILES = 528


def block_levels(key, shape, pieces, least, top_value):
    loudness, own = 1.0, jax.random.fold_in(key, 6)
    for dim, shards_of in pieces:
        steps = jnp.exp(jax.random.uniform(jax.random.fold_in(own, dim), (shards_of,), jnp.float32, least / len(pieces), top_value / len(pieces)))
        loudness = loudness * jnp.repeat(steps, shape[dim] // shards_of).reshape([-1 if axis == dim else 1 for axis in range(len(shape))])
    return loudness


def gaussian(key, shape, scale, limit, pieces=(), kind=jnp.bfloat16):
    values = scale * jax.random.normal(key, shape, jnp.float32)
    if pieces:
        values = values * block_levels(key, shape, pieces, -0.22, 0.18)
    return jnp.clip(values, -limit, limit).astype(kind)


def setup_inputs(seed: int = 0, part: int = 0) -> dict:
    streams_of = jax.random.split(jax.random.key(seed), 5)
    part_keys = jax.random.split(jax.random.fold_in(streams_of[4], part), 5)
    green = gaussian(part_keys[0], (NPTS, 2 * NS), (NPTS ** -0.25), 0.52734375, ((0, 16),))
    log_strength = jnp.clip(jax.random.uniform(part_keys[1], (NPTS,), jnp.float32, -1.0, 1.0) * block_levels(part_keys[1], (NPTS,), ((0, 16),), -0.4, 0.0), -1.0, 1.0)
    observed = gaussian(part_keys[2], (TILES, 2 * B * B), 1.0, 6.0, (), jnp.float32)
    owner_map = jax.random.permutation(part_keys[3], TILES).astype(jnp.int32)
    return {"green": green, "log_strength": log_strength, "observed": observed, "owner_map": owner_map}


def upper_index(blocks):
    rows, cols = np.triu_indices(blocks)
    return jnp.asarray(rows * blocks + cols, dtype=jnp.int32)


def tile_spectra(green, strength, blocks):
    stations = green.shape[1] // 2
    width = stations // blocks
    weighted = (green.astype(jnp.float32) * strength[:, None]).astype(jnp.bfloat16)
    product = lax.dot_general(weighted, green, (((0,), (0,)), ((), ())), preferred_element_type=jnp.float32)
    real_part = product[:stations, :stations] + product[stations:, stations:]
    imag_part = product[stations:, :stations] - product[:stations, stations:]
    picked = upper_index(blocks)

    def to_tiles(matrix):
        return matrix.reshape(blocks, width, blocks, width).transpose(0, 2, 1, 3).reshape(blocks * blocks, width * width)

    return jnp.concatenate([to_tiles(real_part)[picked], to_tiles(imag_part)[picked]], axis=1)


def contraction(green, kernel_tiles, blocks):
    stations = green.shape[1] // 2
    width = stations // blocks
    full_tiles = jnp.zeros((blocks * blocks, 2 * width * width), jnp.bfloat16).at[upper_index(blocks)].set(kernel_tiles)

    def to_matrix(flat):
        return flat.reshape(blocks, blocks, width, width).transpose(0, 2, 1, 3).reshape(stations, stations)

    real_part = to_matrix(full_tiles[:, :width * width])
    imag_part = to_matrix(full_tiles[:, width * width:])
    kernel = jnp.concatenate([jnp.concatenate([real_part, -imag_part], axis=1), jnp.concatenate([imag_part, real_part], axis=1)], axis=0)
    mapped = jnp.dot(green, kernel, preferred_element_type=jnp.float32)
    return jnp.sum(green.astype(jnp.float32) * mapped, axis=1)


def reference(green, log_strength, observed, owner_map):
    log_now = log_strength
    tile_residual = observed
    for iteration in range(STEPS):
        strength = jnp.exp(log_now)
        spectra_tiles = tile_spectra(green, strength, NB)
        tile_residual = jnp.tanh(spectra_tiles - observed)
        kernel_tiles = tile_residual.astype(jnp.bfloat16)
        log_now = log_now - 0.5 * strength * contraction(green, kernel_tiles, NB)
    return log_now, tile_residual[owner_map]
```

```python
import functools

import jax
import jax.numpy as jnp
import numpy as np
from jax import lax
from jax.experimental import pallas as pl
from jax.experimental.pallas import tpu as pltpu
from jax.sharding import PartitionSpec as P

NB = 32
STEPS = 2
LANES = 128
MESH = pl.DeviceIdType.MESH
F32, BF16 = jnp.float32, jnp.bfloat16


def upper_blocks(count):
    return [(g, c) for g in range(count) for c in range(g, count)]


def slot_table(blocks, width):
    per_lane = LANES // width
    index = {gc: b for b, gc in enumerate(upper_blocks(blocks * width // LANES))}
    rows, cols = np.triu_indices(blocks)
    units = [index[(i // per_lane, j // per_lane)] * per_lane + i % per_lane for i, j in zip(rows, cols)]
    return np.asarray(units, np.int32), np.asarray(cols % per_lane, np.int32)


def pieces(axis_sizes, units):
    n_wide, n_narrow, n_tile = axis_sizes
    total = n_wide * n_narrow * n_tile
    return -(-units // total)


def kernel(
    sizes, send_types,
    green_ref, log_ref, observed_ref, owner_ref, unit_ref, lane_ref,
    new_log_ref, out_ref,
    green_t, weighted_t, spectra, half, half_send, quarter, quarter_send, own_observed,
    re_kernel, im_kernel, gathered, gathered_low, staged_re, staged_im,
    recv_tile, recv_narrow, recv_wide,
    rs_send, rs_recv, ag_send, ag_recv,
):
    n_wide, n_narrow, n_tile = sizes
    ns = green_ref.shape[1] // 2
    width = ns // NB
    per_lane = LANES // width
    blocks = upper_blocks(ns // LANES)
    re_units = len(blocks) * per_lane
    flat = width * width
    per = pieces(sizes, 2 * re_units)
    w, n, t = lax.axis_index("wide"), lax.axis_index("narrow"), lax.axis_index("tile")
    axes = (("tile", n_tile, t), ("narrow", n_narrow, n), ("wide", n_wide, w))

    barrier = pltpu.get_barrier_semaphore()
    for name, size, me in axes:
        for o in range(1, size):
            pl.semaphore_signal(barrier, inc=1, device_id={name: lax.rem(me + o, size)}, device_id_type=MESH)
    pl.semaphore_wait(barrier, n_tile + n_narrow + n_wide - 3)

    green_t[...] = green_ref[...].T

    narrow_units = n_wide * per
    tile_units = n_narrow * narrow_units
    my_quarter = t * tile_units + n * narrow_units
    my_first = my_quarter + w * per

    def unit_facts(u):
        part = jnp.where(u >= re_units, 1, 0) + jnp.where(u >= 2 * re_units, 1, 0)
        v = jnp.where(part == 2, 0, u - part * re_units)
        b = v // per_lane
        g, c = jnp.int32(0), b
        first = 0
        for row in range(1, ns // LANES):
            first += ns // LANES - row + 1
            g = jnp.where(b >= first, row, g)
            c = jnp.where(b >= first, b - first + row, c)
        return part, g * per_lane + v % per_lane, c

    lane = lax.broadcasted_iota(jnp.int32, (width, per_lane, LANES), 2)
    place = lax.broadcasted_iota(jnp.int32, (width, per_lane, LANES), 1)
    in_place = lane // width == place
    entry = lax.broadcasted_iota(jnp.int32, (width, per_lane, flat), 2)
    row_of = lax.broadcasted_iota(jnp.int32, (width, per_lane, flat), 0)
    in_row = entry // width == row_of
    fold_a = lax.broadcasted_iota(jnp.int32, (flat, LANES), 0)
    fold_b = lax.broadcasted_iota(jnp.int32, (flat, LANES), 1)
    fold = jnp.where(fold_a % width == fold_b % width, 1.0, 0.0).astype(BF16)

    for e in range(per):
        part, i, c = unit_facts(my_first + e)
        start = i * NB - (i * (i - 1)) // 2 + c * per_lane - i
        both = jnp.concatenate([observed_ref[pl.ds(start + j, 1), :] for j in range(per_lane)], axis=0)
        tiles = jnp.where(part == 1, both[:, flat:], both[:, :flat])
        spread = jnp.where(in_row, tiles[None], 0.0).reshape(width * per_lane, flat)
        high = spread.astype(BF16)
        low = (spread - high.astype(F32)).astype(BF16)
        lanes = jnp.dot(high, fold, preferred_element_type=F32) + jnp.dot(low, fold, preferred_element_type=F32)
        own_observed[e] = jnp.sum(jnp.where(in_place, lanes.reshape(width, per_lane, LANES), 0.0), axis=1)

    for ref in (re_kernel, im_kernel):
        ref[...] = jnp.zeros_like(ref)
    pad_units = spectra.shape[0] - 2 * re_units
    if pad_units:
        spectra[2 * re_units:] = jnp.zeros((pad_units, width, LANES), F32)

    wide_rows = 2 * LANES
    row_groups = [(r, slice(r, r + wide_rows)) for r in range(0, ns, wide_rows)]

    def copies(src_of, dst_of, name, size, me, send, recv, base):
        out = []
        for o in range(1, size):
            to = lax.rem(me + o, size)
            out.append(pltpu.make_async_remote_copy(
                src_ref=src_of(to), dst_ref=dst_of(o), send_sem=send.at[base + o - 1], recv_sem=recv.at[base + o - 1],
                device_id={name: to}, device_id_type=MESH))
        for copy in out:
            copy.start()
        return out

    def wait(started):
        for copy in started:
            copy.wait()

    per_pass = n_tile + n_narrow + n_wide - 3
    at_narrow, at_wide = n_tile - 1, n_tile + n_narrow - 2
    log_now = log_ref[...]
    for step in range(STEPS):
        last = step == STEPS - 1
        strength = jnp.exp(log_now)
        weighted_t[...] = (green_t[...].astype(F32) * strength).astype(BF16)
        for r, rows in row_groups:
            rows_b = slice(ns + r, ns + r + wide_rows)
            wa, wb = weighted_t[rows, :], weighted_t[rows_b, :]
            ga, gb = green_ref[:, r:ns], green_ref[:, ns + r:]
            real = jnp.dot(wa, ga, preferred_element_type=F32) + jnp.dot(wb, gb, preferred_element_type=F32)
            imag = jnp.dot(wb, ga, preferred_element_type=F32) - jnp.dot(wa, gb, preferred_element_type=F32)
            for b, (g, c) in enumerate(blocks):
                if r <= g * LANES < r + wide_rows:
                    at = (slice(g * LANES - r, (g + 1) * LANES - r), slice(c * LANES - r, (c + 1) * LANES - r))
                    spectra[b * per_lane:(b + 1) * per_lane] = real[at].reshape(per_lane, width, LANES)
                    first = re_units + b * per_lane
                    spectra[first:first + per_lane] = imag[at].reshape(per_lane, width, LANES)

        base = step * per_pass
        wait(copies(
            lambda to: spectra.at[pl.ds(to * tile_units, tile_units)], lambda o: recv_tile.at[step, o - 1],
            "tile", n_tile, t, rs_send, rs_recv, base))
        total = spectra[pl.ds(t * tile_units, tile_units)]
        for o in range(n_tile - 1):
            total = total + recv_tile[step, o]
        half[...] = total
        source = half_send[step] if half_send[step] is not None else half
        if source is not half:
            source[...] = total.astype(source.dtype)
        wait(copies(
            lambda to: source.at[pl.ds(to * narrow_units, narrow_units)], lambda o: recv_narrow[step].at[o - 1],
            "narrow", n_narrow, n, rs_send, rs_recv, base + at_narrow))
        total = half[pl.ds(n * narrow_units, narrow_units)]
        for o in range(n_narrow - 1):
            total = total + recv_narrow[step][o].astype(F32)
        quarter[...] = total
        source = quarter_send[step] if quarter_send[step] is not None else quarter
        if source is not quarter:
            source[...] = total.astype(source.dtype)
        wait(copies(
            lambda to: source.at[pl.ds(to * per, per)], lambda o: recv_wide[step].at[o - 1],
            "wide", n_wide, w, rs_send, rs_recv, base + at_wide))
        total = quarter[pl.ds(w * per, per)]
        for o in range(n_wide - 1):
            total = total + recv_wide[step][o].astype(F32)
        residual = jnp.tanh(total - own_observed[...])

        column = lax.broadcasted_iota(jnp.int32, (width, LANES), 1) // width
        kept = []
        for e in range(per):
            part, i, c = unit_facts(my_first + e)
            limit = jnp.where(part == 2, NB, i)
            kept.append(jnp.where(column + c * per_lane >= limit, residual[e], 0.0))
        residual = jnp.stack(kept)
        high = residual.astype(BF16)
        mine = pl.ds(my_first, per)
        gathered[step, mine] = high
        if last:
            gathered_low[mine] = (residual - high.astype(F32)).astype(BF16)

        def gather(ref, name, size, me, first, units, at):
            view = ref.at[pl.ds(first, units)]
            return copies(lambda to: view, lambda o: view, name, size, me, ag_send, ag_recv, at)

        hi = gathered.at[step]
        base_low = STEPS * per_pass
        run = gather(hi, "wide", n_wide, w, my_first, per, base + at_wide)
        if last:
            low_run = gather(gathered_low, "wide", n_wide, w, my_first, per, base_low + at_wide)
        wait(run)
        wait(gather(hi, "narrow", n_narrow, n, my_quarter, narrow_units, base + at_narrow))
        run = gather(hi, "tile", n_tile, t, t * tile_units, tile_units, base)
        if last:
            wait(low_run)
            low_run = gather(gathered_low, "narrow", n_narrow, n, my_quarter, narrow_units, base_low + at_narrow)
        wait(run)

        for b, (g, c) in enumerate(blocks):
            at = (slice(g * LANES, (g + 1) * LANES), slice(c * LANES, (c + 1) * LANES))
            re_kernel[at] = gathered[step, b * per_lane:(b + 1) * per_lane].reshape(LANES, LANES)
            first = re_units + b * per_lane
            im_kernel[at] = gathered[step, first:first + per_lane].reshape(LANES, LANES)
        contraction = jnp.zeros_like(log_now)
        for r, rows in row_groups:
            rows_b = slice(ns + r, ns + r + wide_rows)
            a, b = green_t[r:ns, :], green_t[ns + r:, :]
            re, im = re_kernel[rows, r:ns], im_kernel[rows, r:ns]
            top = jnp.dot(re, a, preferred_element_type=F32) - jnp.dot(im, b, preferred_element_type=F32)
            bottom = jnp.dot(im, a, preferred_element_type=F32) + jnp.dot(re, b, preferred_element_type=F32)
            terms = green_t[rows, :].astype(F32) * top + green_t[rows_b, :].astype(F32) * bottom
            contraction = contraction + jnp.sum(terms, axis=0, keepdims=True)
        log_now = log_now - 0.5 * strength * contraction

    new_log_ref[...] = log_now
    wait(low_run)
    wait(gather(gathered_low, "tile", n_tile, t, t * tile_units, tile_units, base_low))

    slots = out_ref.shape[0]
    lane_group = lax.broadcasted_iota(jnp.int32, (width, LANES), 1) // width

    def stage(k, carry):
        tile = owner_ref[w * slots + k]
        unit, group = unit_ref[tile], lane_ref[tile]
        keep = lane_group == group
        for ref, offset in ((staged_re, 0), (staged_im, re_units)):
            for part, source in enumerate((gathered.at[STEPS - 1], gathered_low)):
                value = jnp.where(keep, source[unit + offset].astype(F32), 0.0)
                ref[k, :, part * LANES:(part + 1) * LANES] = value.astype(BF16)
        return carry

    lax.fori_loop(0, slots, stage, 0)
    unfold_a = lax.broadcasted_iota(jnp.int32, (2 * LANES, flat), 0)
    unfold_b = lax.broadcasted_iota(jnp.int32, (2 * LANES, flat), 1)
    unfold = jnp.where(unfold_a % width == unfold_b % width, 1.0, 0.0).astype(BF16)
    row = lax.broadcasted_iota(jnp.int32, (1, width, flat), 1)
    col = lax.broadcasted_iota(jnp.int32, (1, width, flat), 2)
    diagonal = col // width == row
    for part, ref in enumerate((staged_re, staged_im)):
        rows = ref[...].reshape(slots * width, 2 * LANES)
        spread = jnp.dot(rows, unfold, preferred_element_type=F32).reshape(slots, width, flat)
        out_ref[:, part * flat:(part + 1) * flat] = jnp.sum(jnp.where(diagonal, spread, 0.0), axis=1)


def solution(mesh):
    sizes = (mesh.shape["wide"], mesh.shape["narrow"], mesh.shape["tile"])
    n_wide, n_narrow, n_tile = sizes
    send_types = (F32,) * STEPS

    def on_device(green, log_strength, observed, owner_map):
        points, stations = green.shape
        ns = stations // 2
        width = ns // NB
        flat = width * width
        per_lane = LANES // width
        slots = owner_map.shape[0] // n_wide
        units = 2 * len(upper_blocks(ns // LANES)) * per_lane
        per = pieces(sizes, units)
        narrow_units = n_wide * per
        tile_units = n_narrow * narrow_units
        all_units = n_tile * tile_units
        per_pass = n_tile + n_narrow + n_wide - 3

        def buf(lead, kind):
            return pltpu.VMEM((*lead, width, LANES), kind)

        vmem, smem = pl.BlockSpec(memory_space=pltpu.VMEM), pl.BlockSpec(memory_space=pltpu.SMEM)
        unit_table, lane_table = slot_table(NB, width)
        sems = pltpu.SemaphoreType.DMA
        new_log, residual = pl.pallas_call(
            functools.partial(kernel, sizes, send_types),
            out_shape=(
                jax.ShapeDtypeStruct((1, points), F32),
                jax.ShapeDtypeStruct((slots, 2 * flat), F32),
            ),
            in_specs=[vmem] * 3 + [smem] * 3,
            out_specs=(vmem, vmem),
            scratch_shapes=[
                pltpu.VMEM((stations, points), BF16),
                pltpu.VMEM((stations, points), BF16),
                buf((all_units,), F32),
                buf((tile_units,), F32),
                tuple(None if k == F32 else buf((tile_units,), k) for k in send_types),
                buf((narrow_units,), F32),
                tuple(None if k == F32 else buf((narrow_units,), k) for k in send_types),
                buf((per,), F32),
                pltpu.VMEM((ns, ns), BF16),
                pltpu.VMEM((ns, ns), BF16),
                buf((STEPS, all_units), BF16),
                buf((all_units,), BF16),
                pltpu.VMEM((slots, width, 2 * LANES), BF16),
                pltpu.VMEM((slots, width, 2 * LANES), BF16),
                buf((STEPS, n_tile - 1, tile_units), F32),
                tuple(buf((n_narrow - 1, narrow_units), k) for k in send_types),
                tuple(buf((n_wide - 1, per), k) for k in send_types),
                sems((STEPS * per_pass,)),
                sems((STEPS * per_pass,)),
                sems(((STEPS + 1) * per_pass,)),
                sems(((STEPS + 1) * per_pass,)),
            ],
            compiler_params=pltpu.CompilerParams(
                collective_id=0, has_side_effects=True, vmem_limit_bytes=60 * 1024 * 1024
            ),
        )(green, log_strength[None, :], observed, owner_map, jnp.asarray(unit_table), jnp.asarray(lane_table))
        return new_log[0], residual

    parts = ("grp", "wide", "narrow", "tile")
    return jax.shard_map(
        on_device, mesh=mesh, in_specs=(P(parts, None), P(parts), P("grp", None), P("grp")),
        out_specs=(P(parts), P(("grp", "wide"), None)), check_vma=False,
    )
```

```python
import functools

import jax
import jax.numpy as jnp
import numpy as np
from jax import lax
from jax.experimental import pallas as pl
from jax.experimental.pallas import tpu as pltpu
from jax.sharding import PartitionSpec as P

NB = 32
STEPS = 2
LANES = 128
MESH = pl.DeviceIdType.MESH
F32, BF16 = jnp.float32, jnp.bfloat16


def upper_blocks(count):
    return [(g, c) for g in range(count) for c in range(g, count)]


def slot_table(blocks, width):
    per_lane = LANES // width
    index = {gc: b for b, gc in enumerate(upper_blocks(blocks * width // LANES))}
    rows, cols = np.triu_indices(blocks)
    units = [index[(i // per_lane, j // per_lane)] * per_lane + i % per_lane for i, j in zip(rows, cols)]
    return np.asarray(units, np.int32), np.asarray(cols % per_lane, np.int32)


def piece_units(sizes, units):
    n_wide, n_narrow, n_tile = sizes
    return -(-units // (n_wide * n_narrow * n_tile))


def kernel(
    sizes,
    green_ref, log_ref, observed_ref, owner_ref, unit_ref, lane_ref,
    new_log_ref, out_ref,
    green_t, weighted_t, spectra, half, half_send, quarter, quarter_send, own_observed,
    kernels, gathered, gathered_low, staged_re, staged_im,
    recv_tile, recv_narrow, recv_wide,
    rs_send, rs_recv, ag_send, ag_recv,
):
    n_wide, n_narrow, n_tile = sizes
    ns = green_ref.shape[1] // 2
    width = ns // NB
    per_lane = LANES // width
    blocks = upper_blocks(ns // LANES)
    units = len(blocks) * per_lane
    flat = width * width
    per = piece_units(sizes, units)
    w, n, t = lax.axis_index("wide"), lax.axis_index("narrow"), lax.axis_index("tile")
    places = {"tile": (n_tile, t), "narrow": (n_narrow, n), "wide": (n_wide, w)}

    barrier = pltpu.get_barrier_semaphore()
    for name, (size, me) in places.items():
        for o in range(1, size):
            pl.semaphore_signal(barrier, inc=1, device_id={name: lax.rem(me + o, size)}, device_id_type=MESH)
    pl.semaphore_wait(barrier, n_tile + n_narrow + n_wide - 3)

    green_t[...] = green_ref[...].T

    narrow_units = n_wide * per
    tile_units = n_narrow * narrow_units
    my_tile = t * tile_units
    my_quarter = my_tile + n * narrow_units
    my_first = my_quarter + w * per

    def unit_facts(u):
        padding = u >= units
        v = jnp.where(padding, 0, u)
        b = v // per_lane
        g, c = jnp.int32(0), b
        first = 0
        for row in range(1, ns // LANES):
            first += ns // LANES - row + 1
            g = jnp.where(b >= first, row, g)
            c = jnp.where(b >= first, b - first + row, c)
        return padding, g * per_lane + v % per_lane, c

    def lay_out_observed():
        lane = lax.broadcasted_iota(jnp.int32, (width, per_lane, LANES), 2)
        place = lax.broadcasted_iota(jnp.int32, (width, per_lane, LANES), 1)
        in_place = lane // width == place
        entry = lax.broadcasted_iota(jnp.int32, (width, per_lane, flat), 2)
        row_of = lax.broadcasted_iota(jnp.int32, (width, per_lane, flat), 0)
        in_row = entry // width == row_of
        fold_a = lax.broadcasted_iota(jnp.int32, (flat, LANES), 0)
        fold_b = lax.broadcasted_iota(jnp.int32, (flat, LANES), 1)
        fold = jnp.where(fold_a % width == fold_b % width, 1.0, 0.0).astype(BF16)
        for e in range(per):
            _, i, c = unit_facts(my_first + e)
            start = i * NB - (i * (i - 1)) // 2 + c * per_lane - i
            both = jnp.concatenate([observed_ref[pl.ds(start + j, 1), :] for j in range(per_lane)], axis=0)
            for part in range(2):
                tiles = both[:, part * flat:(part + 1) * flat]
                spread = jnp.where(in_row, tiles[None], 0.0).reshape(width * per_lane, flat)
                high = spread.astype(BF16)
                low = (spread - high.astype(F32)).astype(BF16)
                lanes = jnp.dot(high, fold, preferred_element_type=F32) + jnp.dot(low, fold, preferred_element_type=F32)
                lanes = lanes.reshape(width, per_lane, LANES)
                own_observed[part, e] = jnp.sum(jnp.where(in_place, lanes, 0.0), axis=1)

    wide_rows = 2 * LANES
    row_groups = [(r, slice(r, r + wide_rows)) for r in range(0, ns, wide_rows)]
    per_pass = n_tile + n_narrow + n_wide - 3
    offsets = {"tile": 0, "narrow": n_tile - 1, "wide": n_tile + n_narrow - 2}
    pending = []

    def copies(src_of, dst_of, name, send, recv, group):
        size, me = places[name]
        base = group * per_pass + offsets[name] - 1
        out = []
        for o in range(1, size):
            to = lax.rem(me + o, size)
            out.append(pltpu.make_async_remote_copy(
                src_ref=src_of(to), dst_ref=dst_of(o), send_sem=send.at[base + o], recv_sem=recv.at[base + o],
                device_id={name: to}, device_id_type=MESH))
        for copy in out:
            copy.start()
        pending.extend(out)
        return out

    def arrive(started):
        for copy in started:
            copy.wait_recv()

    def gather(ref, name, group):
        first, count = {
            "wide": (my_first, per), "narrow": (my_quarter, narrow_units), "tile": (my_tile, tile_units),
        }[name]
        view = ref.at[pl.ds(first, count)]
        return copies(lambda to: view, lambda o: view, name, ag_send, ag_recv, group)

    log_now = log_ref[...]
    for step in range(STEPS):
        last = step == STEPS - 1
        strength = jnp.exp(log_now)
        weighted_t[...] = (green_t[...].astype(F32) * strength).astype(BF16)
        run = [None, None]
        for part in range(2):
            for r, rows in row_groups:
                wa, wb = weighted_t[rows, :], weighted_t[slice(ns + r, ns + r + wide_rows), :]
                ga, gb = green_ref[:, r:ns], green_ref[:, ns + r:]
                if part == 0:
                    value = jnp.dot(wa, ga, preferred_element_type=F32) + jnp.dot(wb, gb, preferred_element_type=F32)
                else:
                    value = jnp.dot(wb, ga, preferred_element_type=F32) - jnp.dot(wa, gb, preferred_element_type=F32)
                for b, (g, c) in enumerate(blocks):
                    if r <= g * LANES < r + wide_rows:
                        at = (slice(g * LANES - r, (g + 1) * LANES - r), slice(c * LANES - r, (c + 1) * LANES - r))
                        spectra[part, b * per_lane:(b + 1) * per_lane] = value[at].reshape(per_lane, width, LANES)
            pad_units = spectra.shape[1] - units
            if pad_units and step == 0:
                spectra[part, units:] = jnp.zeros((pad_units, width, LANES), F32)
            run[part] = copies(
                lambda to: spectra.at[part, pl.ds(to * tile_units, tile_units)], lambda o: recv_tile.at[step, part, o - 1],
                "tile", rs_send, rs_recv, 2 * step + part)
        if step == 0:
            lay_out_observed()
            kernels[...] = jnp.zeros_like(kernels)
        for part in range(2):
            arrive(run[part])
            total = spectra[part, pl.ds(my_tile, tile_units)]
            for o in range(n_tile - 1):
                total = total + recv_tile[step, part, o]
            half[part] = total
            source = half
            if half_send[step] is not None:
                source = half_send[step]
                source[part] = total.astype(source.dtype)
            run[part] = copies(
                lambda to: source.at[part, pl.ds(to * narrow_units, narrow_units)],
                lambda o: recv_narrow[step].at[part, o - 1], "narrow", rs_send, rs_recv, 2 * step + part)
        for part in range(2):
            arrive(run[part])
            total = half[part, pl.ds(n * narrow_units, narrow_units)]
            for o in range(n_narrow - 1):
                total = total + recv_narrow[step][part, o].astype(F32)
            quarter[part] = total
            source = quarter
            if quarter_send[step] is not None:
                source = quarter_send[step]
                source[part] = total.astype(source.dtype)
            run[part] = copies(
                lambda to: source.at[part, pl.ds(to * per, per)],
                lambda o: recv_wide[step].at[part, o - 1], "wide", rs_send, rs_recv, 2 * step + part)
        column = lax.broadcasted_iota(jnp.int32, (width, LANES), 1) // width
        for part in range(2):
            arrive(run[part])
            total = quarter[part, pl.ds(w * per, per)]
            for o in range(n_wide - 1):
                total = total + recv_wide[step][part, o].astype(F32)
            residual = jnp.tanh(total - own_observed[part])
            kept = []
            for e in range(per):
                padding, i, c = unit_facts(my_first + e)
                limit = jnp.where(padding, NB, i)
                kept.append(jnp.where(column + c * per_lane >= limit, residual[e], 0.0))
            residual = jnp.stack(kept)
            high = residual.astype(BF16)
            gathered[step, part, pl.ds(my_first, per)] = high
            if last:
                gathered_low[part, pl.ds(my_first, per)] = (residual - high.astype(F32)).astype(BF16)
            run[part] = gather(gathered.at[step, part], "wide", 2 * step + part)
        low_run = [None, None]

        def low_stage(name):
            if last:
                for part in range(2):
                    if low_run[part] is not None:
                        arrive(low_run[part])
                    low_run[part] = gather(gathered_low.at[part], name, 2 * STEPS + part)

        low_stage("wide")
        for name in ("narrow", "tile"):
            for part in range(2):
                arrive(run[part])
                run[part] = gather(gathered.at[step, part], name, 2 * step + part)
        contraction = jnp.zeros_like(log_now)
        for part in range(2):
            arrive(run[part])
            low_stage(("narrow", "tile")[part])
            for b, (g, c) in enumerate(blocks):
                at = (slice(g * LANES, (g + 1) * LANES), slice(c * LANES, (c + 1) * LANES))
                kernels[(part, *at)] = gathered[step, part, b * per_lane:(b + 1) * per_lane].reshape(LANES, LANES)
            for r, rows in row_groups:
                block = kernels[part, rows, r:ns]
                from_a = jnp.dot(block, green_t[r:ns, :], preferred_element_type=F32)
                from_b = jnp.dot(block, green_t[ns + r:, :], preferred_element_type=F32)
                a = green_t[rows, :].astype(F32)
                b = green_t[slice(ns + r, ns + r + wide_rows), :].astype(F32)
                terms = a * from_a + b * from_b if part == 0 else b * from_a - a * from_b
                contraction = contraction + jnp.sum(terms, axis=0, keepdims=True)
        log_now = log_now - 0.5 * strength * contraction
        for copy in pending:
            copy.wait_send()
        pending.clear()

    new_log_ref[...] = log_now
    for part in range(2):
        arrive(low_run[part])

    slots = out_ref.shape[0]
    lane_group = lax.broadcasted_iota(jnp.int32, (width, LANES), 1) // width

    def stage(k, carry):
        tile = owner_ref[w * slots + k]
        unit, group = unit_ref[tile], lane_ref[tile]
        keep = lane_group == group
        for part, ref in enumerate((staged_re, staged_im)):
            for side, source in enumerate((gathered.at[STEPS - 1, part], gathered_low.at[part])):
                value = jnp.where(keep, source[unit].astype(F32), 0.0)
                ref[k, :, side * LANES:(side + 1) * LANES] = value.astype(BF16)
        return carry

    lax.fori_loop(0, slots, stage, 0)
    unfold_a = lax.broadcasted_iota(jnp.int32, (2 * LANES, flat), 0)
    unfold_b = lax.broadcasted_iota(jnp.int32, (2 * LANES, flat), 1)
    unfold = jnp.where(unfold_a % width == unfold_b % width, 1.0, 0.0).astype(BF16)
    row = lax.broadcasted_iota(jnp.int32, (1, width, flat), 1)
    col = lax.broadcasted_iota(jnp.int32, (1, width, flat), 2)
    diagonal = col // width == row
    for part, ref in enumerate((staged_re, staged_im)):
        rows = ref[...].reshape(slots * width, 2 * LANES)
        spread = jnp.dot(rows, unfold, preferred_element_type=F32).reshape(slots, width, flat)
        out_ref[:, part * flat:(part + 1) * flat] = jnp.sum(jnp.where(diagonal, spread, 0.0), axis=1)


def solution(mesh):
    sizes = (mesh.shape["wide"], mesh.shape["narrow"], mesh.shape["tile"])
    n_wide, n_narrow, n_tile = sizes
    send_types = (F32,) * STEPS

    def on_device(green, log_strength, observed, owner_map):
        points, stations = green.shape
        ns = stations // 2
        width = ns // NB
        flat = width * width
        per_lane = LANES // width
        slots = owner_map.shape[0] // n_wide
        units = len(upper_blocks(ns // LANES)) * per_lane
        per = piece_units(sizes, units)
        narrow_units = n_wide * per
        tile_units = n_narrow * narrow_units
        all_units = n_tile * tile_units
        per_pass = n_tile + n_narrow + n_wide - 3

        def buf(lead, kind):
            return pltpu.VMEM((*lead, width, LANES), kind)

        vmem, smem = pl.BlockSpec(memory_space=pltpu.VMEM), pl.BlockSpec(memory_space=pltpu.SMEM)
        unit_table, lane_table = slot_table(NB, width)
        sems = pltpu.SemaphoreType.DMA
        new_log, residual = pl.pallas_call(
            functools.partial(kernel, sizes),
            out_shape=(
                jax.ShapeDtypeStruct((1, points), F32),
                jax.ShapeDtypeStruct((slots, 2 * flat), F32),
            ),
            in_specs=[vmem] * 3 + [smem] * 3,
            out_specs=(vmem, vmem),
            scratch_shapes=[
                pltpu.VMEM((stations, points), BF16),
                pltpu.VMEM((stations, points), BF16),
                buf((2, all_units), F32),
                buf((2, tile_units), F32),
                tuple(None if k == F32 else buf((2, tile_units), k) for k in send_types),
                buf((2, narrow_units), F32),
                tuple(None if k == F32 else buf((2, narrow_units), k) for k in send_types),
                buf((2, per), F32),
                pltpu.VMEM((2, ns, ns), BF16),
                buf((STEPS, 2, all_units), BF16),
                buf((2, all_units), BF16),
                pltpu.VMEM((slots, width, 2 * LANES), BF16),
                pltpu.VMEM((slots, width, 2 * LANES), BF16),
                buf((STEPS, 2, n_tile - 1, tile_units), F32),
                tuple(buf((2, n_narrow - 1, narrow_units), k) for k in send_types),
                tuple(buf((2, n_wide - 1, per), k) for k in send_types),
                sems((2 * STEPS * per_pass,)),
                sems((2 * STEPS * per_pass,)),
                sems((2 * (STEPS + 1) * per_pass,)),
                sems((2 * (STEPS + 1) * per_pass,)),
            ],
            compiler_params=pltpu.CompilerParams(
                collective_id=0, has_side_effects=True, vmem_limit_bytes=60 * 1024 * 1024
            ),
        )(green, log_strength[None, :], observed, owner_map, jnp.asarray(unit_table), jnp.asarray(lane_table))
        return new_log[0], residual

    parts = ("grp", "wide", "narrow", "tile")
    return jax.shard_map(
        on_device, mesh=mesh, in_specs=(P(parts, None), P(parts), P("grp", None), P("grp")),
        out_specs=(P(parts), P(("grp", "wide"), None)), check_vma=False,
    )
```

```python
import functools

import jax
import jax.numpy as jnp
import numpy as np
from jax import lax
from jax.experimental import pallas as pl
from jax.experimental.pallas import tpu as pltpu
from jax.sharding import PartitionSpec as P

NB = 32
STEPS = 2
LANES = 128
MESH = pl.DeviceIdType.MESH
F32, BF16 = jnp.float32, jnp.bfloat16


def upper_blocks(count):
    return [(g, c) for g in range(count) for c in range(g, count)]


def slot_table(blocks, width):
    per_lane = LANES // width
    index = {gc: b for b, gc in enumerate(upper_blocks(blocks * width // LANES))}
    rows, cols = np.triu_indices(blocks)
    units = [index[(i // per_lane, j // per_lane)] * per_lane + i % per_lane for i, j in zip(rows, cols)]
    return np.asarray(units, np.int32), np.asarray(cols % per_lane, np.int32)


def piece_units(sizes, units):
    n_wide, n_narrow, n_tile = sizes
    return -(-units // (n_wide * n_narrow * n_tile))


def kernel(
    sizes,
    green_ref, log_ref, observed_ref, owner_ref, unit_ref, lane_ref,
    new_log_ref, out_ref,
    green_t, weighted_t, spectra, half, half_send, quarter, quarter_send, own_observed,
    kernels, gathered, gathered_low, staged_re, staged_im,
    recv_tile, recv_narrow, recv_wide,
    rs_send, rs_recv, ag_send, ag_recv,
):
    n_wide, n_narrow, n_tile = sizes
    ns = green_ref.shape[1] // 2
    width = ns // NB
    per_lane = LANES // width
    blocks = upper_blocks(ns // LANES)
    units = len(blocks) * per_lane
    flat = width * width
    per = piece_units(sizes, units)
    w, n, t = lax.axis_index("wide"), lax.axis_index("narrow"), lax.axis_index("tile")
    places = {"tile": (n_tile, t), "narrow": (n_narrow, n), "wide": (n_wide, w)}

    barrier = pltpu.get_barrier_semaphore()
    for name, (size, me) in places.items():
        for o in range(1, size):
            pl.semaphore_signal(barrier, inc=1, device_id={name: lax.rem(me + o, size)}, device_id_type=MESH)
    pl.semaphore_wait(barrier, n_tile + n_narrow + n_wide - 3)

    green_t[...] = green_ref[...].T

    narrow_units = n_wide * per
    tile_units = n_narrow * narrow_units
    my_tile = t * tile_units
    my_quarter = my_tile + n * narrow_units
    my_first = my_quarter + w * per

    def unit_facts(u):
        padding = u >= units
        v = jnp.where(padding, 0, u)
        b = v // per_lane
        g, c = jnp.int32(0), b
        first = 0
        for row in range(1, ns // LANES):
            first += ns // LANES - row + 1
            g = jnp.where(b >= first, row, g)
            c = jnp.where(b >= first, b - first + row, c)
        return padding, g * per_lane + v % per_lane, c

    def lay_out_observed():
        lane = lax.broadcasted_iota(jnp.int32, (width, per_lane, LANES), 2)
        place = lax.broadcasted_iota(jnp.int32, (width, per_lane, LANES), 1)
        in_place = lane // width == place
        entry = lax.broadcasted_iota(jnp.int32, (width, per_lane, flat), 2)
        row_of = lax.broadcasted_iota(jnp.int32, (width, per_lane, flat), 0)
        in_row = entry // width == row_of
        fold_a = lax.broadcasted_iota(jnp.int32, (flat, LANES), 0)
        fold_b = lax.broadcasted_iota(jnp.int32, (flat, LANES), 1)
        fold = jnp.where(fold_a % width == fold_b % width, 1.0, 0.0).astype(BF16)
        for e in range(per):
            _, i, c = unit_facts(my_first + e)
            start = i * NB - (i * (i - 1)) // 2 + c * per_lane - i
            both = jnp.concatenate([observed_ref[pl.ds(start + j, 1), :] for j in range(per_lane)], axis=0)
            for part in range(2):
                tiles = both[:, part * flat:(part + 1) * flat]
                spread = jnp.where(in_row, tiles[None], 0.0).reshape(width * per_lane, flat)
                high = spread.astype(BF16)
                low = (spread - high.astype(F32)).astype(BF16)
                lanes = jnp.dot(high, fold, preferred_element_type=F32) + jnp.dot(low, fold, preferred_element_type=F32)
                lanes = lanes.reshape(width, per_lane, LANES)
                own_observed[part, e] = jnp.sum(jnp.where(in_place, lanes, 0.0), axis=1)

    wide_rows = 2 * LANES
    row_groups = [(r, slice(r, r + wide_rows)) for r in range(0, ns, wide_rows)]
    per_pass = n_tile + n_narrow + n_wide - 3
    offsets = {"tile": 0, "narrow": n_tile - 1, "wide": n_tile + n_narrow - 2}
    pending = []

    def copies(src_of, dst_of, name, send, recv, group):
        size, me = places[name]
        base = group * per_pass + offsets[name] - 1
        out = []
        for o in range(1, size):
            to = lax.rem(me + o, size)
            out.append(pltpu.make_async_remote_copy(
                src_ref=src_of(to), dst_ref=dst_of(o), send_sem=send.at[base + o], recv_sem=recv.at[base + o],
                device_id={name: to}, device_id_type=MESH))
        for copy in out:
            copy.start()
        pending.extend(out)
        return out

    def arrive(started):
        for copy in started:
            copy.wait_recv()

    def gather(ref, name, group):
        first, count = {
            "wide": (my_first, per), "narrow": (my_quarter, narrow_units), "tile": (my_tile, tile_units),
        }[name]
        view = ref.at[pl.ds(first, count)]
        return copies(lambda to: view, lambda o: view, name, ag_send, ag_recv, group)

    log_now = log_ref[...]
    for step in range(STEPS):
        last = step == STEPS - 1
        strength = jnp.exp(log_now)
        weighted_t[...] = (green_t[...].astype(F32) * strength).astype(BF16)
        run = [None, None]
        for part in range(2):
            for r, rows in row_groups:
                wa, wb = weighted_t[rows, :], weighted_t[slice(ns + r, ns + r + wide_rows), :]
                ga, gb = green_ref[:, r:ns], green_ref[:, ns + r:]
                if part == 0:
                    value = jnp.dot(wa, ga, preferred_element_type=F32) + jnp.dot(wb, gb, preferred_element_type=F32)
                else:
                    value = jnp.dot(wb, ga, preferred_element_type=F32) - jnp.dot(wa, gb, preferred_element_type=F32)
                for b, (g, c) in enumerate(blocks):
                    if r <= g * LANES < r + wide_rows:
                        at = (slice(g * LANES - r, (g + 1) * LANES - r), slice(c * LANES - r, (c + 1) * LANES - r))
                        spectra[part, b * per_lane:(b + 1) * per_lane] = value[at].reshape(per_lane, width, LANES)
            pad_units = spectra.shape[1] - units
            if pad_units and step == 0:
                spectra[part, units:] = jnp.zeros((pad_units, width, LANES), F32)
            run[part] = copies(
                lambda to: spectra.at[part, pl.ds(to * tile_units, tile_units)], lambda o: recv_tile.at[step, part, o - 1],
                "tile", rs_send, rs_recv, 2 * step + part)
        if step == 0:
            lay_out_observed()
            kernels[...] = jnp.zeros_like(kernels)
        for part in range(2):
            arrive(run[part])
            total = spectra[part, pl.ds(my_tile, tile_units)]
            for o in range(n_tile - 1):
                total = total + recv_tile[step, part, o]
            half[part] = total
            source = half
            if half_send[step] is not None:
                source = half_send[step]
                source[part] = total.astype(source.dtype)
            run[part] = copies(
                lambda to: source.at[part, pl.ds(to * narrow_units, narrow_units)],
                lambda o: recv_narrow[step].at[part, o - 1], "narrow", rs_send, rs_recv, 2 * step + part)
        for part in range(2):
            arrive(run[part])
            total = half[part, pl.ds(n * narrow_units, narrow_units)]
            for o in range(n_narrow - 1):
                total = total + recv_narrow[step][part, o].astype(F32)
            quarter[part] = total
            source = quarter
            if quarter_send[step] is not None:
                source = quarter_send[step]
                source[part] = total.astype(source.dtype)
            run[part] = copies(
                lambda to: source.at[part, pl.ds(to * per, per)],
                lambda o: recv_wide[step].at[part, o - 1], "wide", rs_send, rs_recv, 2 * step + part)
        column = lax.broadcasted_iota(jnp.int32, (width, LANES), 1) // width
        for part in range(2):
            arrive(run[part])
            total = quarter[part, pl.ds(w * per, per)]
            for o in range(n_wide - 1):
                total = total + recv_wide[step][part, o].astype(F32)
            residual = jnp.tanh(total - own_observed[part])
            kept = []
            for e in range(per):
                padding, i, c = unit_facts(my_first + e)
                limit = jnp.where(padding, NB, i)
                kept.append(jnp.where(column + c * per_lane >= limit, residual[e], 0.0))
            residual = jnp.stack(kept)
            high = residual.astype(BF16)
            gathered[step, part, pl.ds(my_first, per)] = high
            if last:
                gathered_low[part, pl.ds(my_first, per)] = (residual - high.astype(F32)).astype(BF16)
            run[part] = gather(gathered.at[step, part], "wide", 2 * step + part)
        low_run = [None, None]

        def low_stage(name):
            if last:
                for part in range(2):
                    if low_run[part] is not None:
                        arrive(low_run[part])
                    low_run[part] = gather(gathered_low.at[part], name, 2 * STEPS + part)

        low_stage("wide")
        for name in ("narrow", "tile"):
            for part in range(2):
                arrive(run[part])
                run[part] = gather(gathered.at[step, part], name, 2 * step + part)
        contraction = jnp.zeros_like(log_now)
        for part in range(2):
            arrive(run[part])
            low_stage(("narrow", "tile")[part])
            for b, (g, c) in enumerate(blocks):
                at = (slice(g * LANES, (g + 1) * LANES), slice(c * LANES, (c + 1) * LANES))
                kernels[(part, *at)] = gathered[step, part, b * per_lane:(b + 1) * per_lane].reshape(LANES, LANES)
            for r, rows in row_groups:
                block = kernels[part, rows, r:ns]
                from_a = jnp.dot(block, green_t[r:ns, :], preferred_element_type=F32)
                from_b = jnp.dot(block, green_t[ns + r:, :], preferred_element_type=F32)
                a = green_t[rows, :].astype(F32)
                b = green_t[slice(ns + r, ns + r + wide_rows), :].astype(F32)
                terms = a * from_a + b * from_b if part == 0 else b * from_a - a * from_b
                contraction = contraction + jnp.sum(terms, axis=0, keepdims=True)
        log_now = log_now - 0.5 * strength * contraction
        for copy in pending:
            copy.wait_send()
        pending.clear()

    new_log_ref[...] = log_now
    for part in range(2):
        arrive(low_run[part])

    slots = out_ref.shape[0]
    lane_group = lax.broadcasted_iota(jnp.int32, (width, LANES), 1) // width

    def stage(k, carry):
        tile = owner_ref[w * slots + k]
        unit, group = unit_ref[tile], lane_ref[tile]
        keep = lane_group == group
        for part, ref in enumerate((staged_re, staged_im)):
            for side, source in enumerate((gathered.at[STEPS - 1, part], gathered_low.at[part])):
                value = jnp.where(keep, source[unit].astype(F32), 0.0)
                ref[k, :, side * LANES:(side + 1) * LANES] = value.astype(BF16)
        return carry

    lax.fori_loop(0, slots, stage, 0)
    unfold_a = lax.broadcasted_iota(jnp.int32, (2 * LANES, flat), 0)
    unfold_b = lax.broadcasted_iota(jnp.int32, (2 * LANES, flat), 1)
    unfold = jnp.where(unfold_a % width == unfold_b % width, 1.0, 0.0).astype(BF16)
    row = lax.broadcasted_iota(jnp.int32, (1, width, flat), 1)
    col = lax.broadcasted_iota(jnp.int32, (1, width, flat), 2)
    diagonal = col // width == row
    for part, ref in enumerate((staged_re, staged_im)):
        rows = ref[...].reshape(slots * width, 2 * LANES)
        spread = jnp.dot(rows, unfold, preferred_element_type=F32).reshape(slots, width, flat)
        out_ref[:, part * flat:(part + 1) * flat] = jnp.sum(jnp.where(diagonal, spread, 0.0), axis=1)


def solution(mesh):
    sizes = (mesh.shape["wide"], mesh.shape["narrow"], mesh.shape["tile"])
    n_wide, n_narrow, n_tile = sizes
    send_types = (BF16,) * (STEPS - 1) + (F32,)

    def on_device(green, log_strength, observed, owner_map):
        points, stations = green.shape
        ns = stations // 2
        width = ns // NB
        flat = width * width
        per_lane = LANES // width
        slots = owner_map.shape[0] // n_wide
        units = len(upper_blocks(ns // LANES)) * per_lane
        per = piece_units(sizes, units)
        narrow_units = n_wide * per
        tile_units = n_narrow * narrow_units
        all_units = n_tile * tile_units
        per_pass = n_tile + n_narrow + n_wide - 3

        def buf(lead, kind):
            return pltpu.VMEM((*lead, width, LANES), kind)

        vmem, smem = pl.BlockSpec(memory_space=pltpu.VMEM), pl.BlockSpec(memory_space=pltpu.SMEM)
        unit_table, lane_table = slot_table(NB, width)
        sems = pltpu.SemaphoreType.DMA
        new_log, residual = pl.pallas_call(
            functools.partial(kernel, sizes),
            out_shape=(
                jax.ShapeDtypeStruct((1, points), F32),
                jax.ShapeDtypeStruct((slots, 2 * flat), F32),
            ),
            in_specs=[vmem] * 3 + [smem] * 3,
            out_specs=(vmem, vmem),
            scratch_shapes=[
                pltpu.VMEM((stations, points), BF16),
                pltpu.VMEM((stations, points), BF16),
                buf((2, all_units), F32),
                buf((2, tile_units), F32),
                tuple(None if k == F32 else buf((2, tile_units), k) for k in send_types),
                buf((2, narrow_units), F32),
                tuple(None if k == F32 else buf((2, narrow_units), k) for k in send_types),
                buf((2, per), F32),
                pltpu.VMEM((2, ns, ns), BF16),
                buf((STEPS, 2, all_units), BF16),
                buf((2, all_units), BF16),
                pltpu.VMEM((slots, width, 2 * LANES), BF16),
                pltpu.VMEM((slots, width, 2 * LANES), BF16),
                buf((STEPS, 2, n_tile - 1, tile_units), F32),
                tuple(buf((2, n_narrow - 1, narrow_units), k) for k in send_types),
                tuple(buf((2, n_wide - 1, per), k) for k in send_types),
                sems((2 * STEPS * per_pass,)),
                sems((2 * STEPS * per_pass,)),
                sems((2 * (STEPS + 1) * per_pass,)),
                sems((2 * (STEPS + 1) * per_pass,)),
            ],
            compiler_params=pltpu.CompilerParams(
                collective_id=0, has_side_effects=True, vmem_limit_bytes=60 * 1024 * 1024
            ),
        )(green, log_strength[None, :], observed, owner_map, jnp.asarray(unit_table), jnp.asarray(lane_table))
        return new_log[0], residual

    parts = ("grp", "wide", "narrow", "tile")
    return jax.shard_map(
        on_device, mesh=mesh, in_specs=(P(parts, None), P(parts), P("grp", None), P("grp")),
        out_specs=(P(parts), P(("grp", "wide"), None)), check_vma=False,
    )
```

```python
import functools

import jax
import jax.numpy as jnp
import numpy as np
from jax import lax
from jax.experimental import pallas as pl
from jax.experimental.pallas import tpu as pltpu
from jax.sharding import PartitionSpec as P

NB = 32
STEPS = 2
LANES = 128
MESH = pl.DeviceIdType.MESH
F32, BF16 = jnp.float32, jnp.bfloat16


def upper_blocks(count):
    return [(g, c) for g in range(count) for c in range(g, count)]


def slot_table(blocks, width):
    per_lane = LANES // width
    index = {gc: b for b, gc in enumerate(upper_blocks(blocks * width // LANES))}
    rows, cols = np.triu_indices(blocks)
    units = [index[(i // per_lane, j // per_lane)] * per_lane + i % per_lane for i, j in zip(rows, cols)]
    return np.asarray(units, np.int32), np.asarray(cols % per_lane, np.int32)


def piece_units(sizes, units):
    n_wide, n_narrow, n_tile = sizes
    return -(-units // (n_wide * n_narrow * n_tile))


def kernel(
    sizes,
    green_ref, log_ref, observed_ref, owner_ref, unit_ref, lane_ref,
    new_log_ref, out_ref,
    green_t, weighted_t, spectra, spectra_send, half, half_send, quarter, quarter_send, own_observed,
    kernels, gathered, gathered_low, staged_re, staged_im,
    recv_tile, recv_narrow, recv_wide,
    rs_send, rs_recv, ag_send, ag_recv,
):
    n_wide, n_narrow, n_tile = sizes
    ns = green_ref.shape[1] // 2
    width = ns // NB
    per_lane = LANES // width
    blocks = upper_blocks(ns // LANES)
    units = len(blocks) * per_lane
    flat = width * width
    per = piece_units(sizes, units)
    w, n, t = lax.axis_index("wide"), lax.axis_index("narrow"), lax.axis_index("tile")
    places = {"tile": (n_tile, t), "narrow": (n_narrow, n), "wide": (n_wide, w)}

    barrier = pltpu.get_barrier_semaphore()
    for name, (size, me) in places.items():
        for o in range(1, size):
            pl.semaphore_signal(barrier, inc=1, device_id={name: lax.rem(me + o, size)}, device_id_type=MESH)
    pl.semaphore_wait(barrier, n_tile + n_narrow + n_wide - 3)

    green_t[...] = green_ref[...].T

    narrow_units = n_wide * per
    tile_units = n_narrow * narrow_units
    my_tile = t * tile_units
    my_quarter = my_tile + n * narrow_units
    my_first = my_quarter + w * per

    def unit_facts(u):
        padding = u >= units
        v = jnp.where(padding, 0, u)
        b = v // per_lane
        g, c = jnp.int32(0), b
        first = 0
        for row in range(1, ns // LANES):
            first += ns // LANES - row + 1
            g = jnp.where(b >= first, row, g)
            c = jnp.where(b >= first, b - first + row, c)
        return padding, g * per_lane + v % per_lane, c

    def lay_out_observed():
        lane = lax.broadcasted_iota(jnp.int32, (width, per_lane, LANES), 2)
        place = lax.broadcasted_iota(jnp.int32, (width, per_lane, LANES), 1)
        in_place = lane // width == place
        entry = lax.broadcasted_iota(jnp.int32, (width, per_lane, flat), 2)
        row_of = lax.broadcasted_iota(jnp.int32, (width, per_lane, flat), 0)
        in_row = entry // width == row_of
        fold_a = lax.broadcasted_iota(jnp.int32, (flat, LANES), 0)
        fold_b = lax.broadcasted_iota(jnp.int32, (flat, LANES), 1)
        fold = jnp.where(fold_a % width == fold_b % width, 1.0, 0.0).astype(BF16)
        for e in range(per):
            _, i, c = unit_facts(my_first + e)
            start = i * NB - (i * (i - 1)) // 2 + c * per_lane - i
            both = jnp.concatenate([observed_ref[pl.ds(start + j, 1), :] for j in range(per_lane)], axis=0)
            for part in range(2):
                tiles = both[:, part * flat:(part + 1) * flat]
                spread = jnp.where(in_row, tiles[None], 0.0).reshape(width * per_lane, flat)
                high = spread.astype(BF16)
                low = (spread - high.astype(F32)).astype(BF16)
                lanes = jnp.dot(high, fold, preferred_element_type=F32) + jnp.dot(low, fold, preferred_element_type=F32)
                lanes = lanes.reshape(width, per_lane, LANES)
                own_observed[part, e] = jnp.sum(jnp.where(in_place, lanes, 0.0), axis=1)

    wide_rows = 2 * LANES
    row_groups = [(r, slice(r, r + wide_rows)) for r in range(0, ns, wide_rows)]
    per_pass = n_tile + n_narrow + n_wide - 3
    offsets = {"tile": 0, "narrow": n_tile - 1, "wide": n_tile + n_narrow - 2}
    pending = []

    def copies(src_of, dst_of, name, send, recv, group):
        size, me = places[name]
        base = group * per_pass + offsets[name] - 1
        out = []
        for o in range(1, size):
            to = lax.rem(me + o, size)
            out.append(pltpu.make_async_remote_copy(
                src_ref=src_of(to), dst_ref=dst_of(o), send_sem=send.at[base + o], recv_sem=recv.at[base + o],
                device_id={name: to}, device_id_type=MESH))
        for copy in out:
            copy.start()
        pending.extend(out)
        return out

    def arrive(started):
        for copy in started:
            copy.wait_recv()

    def gather(ref, name, group):
        first, count = {
            "wide": (my_first, per), "narrow": (my_quarter, narrow_units), "tile": (my_tile, tile_units),
        }[name]
        view = ref.at[pl.ds(first, count)]
        return copies(lambda to: view, lambda o: view, name, ag_send, ag_recv, group)

    log_now = log_ref[...]
    for step in range(STEPS):
        last = step == STEPS - 1
        strength = jnp.exp(log_now)
        weighted_t[...] = (green_t[...].astype(F32) * strength).astype(BF16)
        run = [None, None]
        first_source = spectra if spectra_send[step] is None else spectra_send[step]
        for part in range(2):
            source = first_source
            for r, rows in row_groups:
                wa, wb = weighted_t[rows, :], weighted_t[slice(ns + r, ns + r + wide_rows), :]
                ga, gb = green_ref[:, r:ns], green_ref[:, ns + r:]
                if part == 0:
                    value = jnp.dot(wa, ga, preferred_element_type=F32) + jnp.dot(wb, gb, preferred_element_type=F32)
                else:
                    value = jnp.dot(wb, ga, preferred_element_type=F32) - jnp.dot(wa, gb, preferred_element_type=F32)
                for b, (g, c) in enumerate(blocks):
                    if r <= g * LANES < r + wide_rows:
                        at = (slice(g * LANES - r, (g + 1) * LANES - r), slice(c * LANES - r, (c + 1) * LANES - r))
                        block = value[at].reshape(per_lane, width, LANES)
                        spectra[part, b * per_lane:(b + 1) * per_lane] = block
                        if source is not spectra:
                            source[part, b * per_lane:(b + 1) * per_lane] = block.astype(source.dtype)
            pad_units = spectra.shape[1] - units
            for ref in {id(r): r for r in (spectra, source)}.values():
                if pad_units and (step == 0 or ref is not spectra):
                    ref[part, units:] = jnp.zeros((pad_units, width, LANES), ref.dtype)
            run[part] = copies(
                lambda to: source.at[part, pl.ds(to * tile_units, tile_units)], lambda o: recv_tile[step].at[part, o - 1],
                "tile", rs_send, rs_recv, 2 * step + part)
        if step == 0:
            lay_out_observed()
            kernels[...] = jnp.zeros_like(kernels)
        for part in range(2):
            arrive(run[part])
            total = spectra[part, pl.ds(my_tile, tile_units)]
            for o in range(n_tile - 1):
                total = total + recv_tile[step][part, o].astype(F32)
            half[part] = total
            source = half
            if half_send[step] is not None:
                source = half_send[step]
                source[part] = total.astype(source.dtype)
            run[part] = copies(
                lambda to: source.at[part, pl.ds(to * narrow_units, narrow_units)],
                lambda o: recv_narrow[step].at[part, o - 1], "narrow", rs_send, rs_recv, 2 * step + part)
        for part in range(2):
            arrive(run[part])
            total = half[part, pl.ds(n * narrow_units, narrow_units)]
            for o in range(n_narrow - 1):
                total = total + recv_narrow[step][part, o].astype(F32)
            quarter[part] = total
            source = quarter
            if quarter_send[step] is not None:
                source = quarter_send[step]
                source[part] = total.astype(source.dtype)
            run[part] = copies(
                lambda to: source.at[part, pl.ds(to * per, per)],
                lambda o: recv_wide[step].at[part, o - 1], "wide", rs_send, rs_recv, 2 * step + part)
        column = lax.broadcasted_iota(jnp.int32, (width, LANES), 1) // width
        for part in range(2):
            arrive(run[part])
            total = quarter[part, pl.ds(w * per, per)]
            for o in range(n_wide - 1):
                total = total + recv_wide[step][part, o].astype(F32)
            residual = jnp.tanh(total - own_observed[part])
            kept = []
            for e in range(per):
                padding, i, c = unit_facts(my_first + e)
                limit = jnp.where(padding, NB, i)
                kept.append(jnp.where(column + c * per_lane >= limit, residual[e], 0.0))
            residual = jnp.stack(kept)
            high = residual.astype(BF16)
            gathered[step, part, pl.ds(my_first, per)] = high
            if last:
                gathered_low[part, pl.ds(my_first, per)] = (residual - high.astype(F32)).astype(BF16)
            run[part] = gather(gathered.at[step, part], "wide", 2 * step + part)
        low_run = [None, None]

        def low_stage(name):
            if last:
                for part in range(2):
                    if low_run[part] is not None:
                        arrive(low_run[part])
                    low_run[part] = gather(gathered_low.at[part], name, 2 * STEPS + part)

        low_stage("wide")
        for name in ("narrow", "tile"):
            for part in range(2):
                arrive(run[part])
                run[part] = gather(gathered.at[step, part], name, 2 * step + part)
        low_stage("narrow")
        contraction = jnp.zeros_like(log_now)
        for part in range(2):
            arrive(run[part])
            for b, (g, c) in enumerate(blocks):
                at = (slice(g * LANES, (g + 1) * LANES), slice(c * LANES, (c + 1) * LANES))
                kernels[(part, *at)] = gathered[step, part, b * per_lane:(b + 1) * per_lane].reshape(LANES, LANES)
            for r, rows in row_groups:
                block = kernels[part, rows, r:ns]
                from_a = jnp.dot(block, green_t[r:ns, :], preferred_element_type=F32)
                from_b = jnp.dot(block, green_t[ns + r:, :], preferred_element_type=F32)
                a = green_t[rows, :].astype(F32)
                b = green_t[slice(ns + r, ns + r + wide_rows), :].astype(F32)
                terms = a * from_a + b * from_b if part == 0 else b * from_a - a * from_b
                contraction = contraction + jnp.sum(terms, axis=0, keepdims=True)
        low_stage("tile")
        log_now = log_now - 0.5 * strength * contraction
        for copy in pending:
            copy.wait_send()
        pending.clear()

    new_log_ref[...] = log_now
    for part in range(2):
        arrive(low_run[part])

    slots = out_ref.shape[0]
    lane_group = lax.broadcasted_iota(jnp.int32, (width, LANES), 1) // width

    def stage(k, carry):
        tile = owner_ref[w * slots + k]
        unit, group = unit_ref[tile], lane_ref[tile]
        keep = lane_group == group
        for part, ref in enumerate((staged_re, staged_im)):
            for side, source in enumerate((gathered.at[STEPS - 1, part], gathered_low.at[part])):
                value = jnp.where(keep, source[unit].astype(F32), 0.0)
                ref[k, :, side * LANES:(side + 1) * LANES] = value.astype(BF16)
        return carry

    lax.fori_loop(0, slots, stage, 0)
    unfold_a = lax.broadcasted_iota(jnp.int32, (2 * LANES, flat), 0)
    unfold_b = lax.broadcasted_iota(jnp.int32, (2 * LANES, flat), 1)
    unfold = jnp.where(unfold_a % width == unfold_b % width, 1.0, 0.0).astype(BF16)
    row = lax.broadcasted_iota(jnp.int32, (1, width, flat), 1)
    col = lax.broadcasted_iota(jnp.int32, (1, width, flat), 2)
    diagonal = col // width == row
    for part, ref in enumerate((staged_re, staged_im)):
        rows = ref[...].reshape(slots * width, 2 * LANES)
        spread = jnp.dot(rows, unfold, preferred_element_type=F32).reshape(slots, width, flat)
        out_ref[:, part * flat:(part + 1) * flat] = jnp.sum(jnp.where(diagonal, spread, 0.0), axis=1)


def solution(mesh):
    sizes = (mesh.shape["wide"], mesh.shape["narrow"], mesh.shape["tile"])
    n_wide, n_narrow, n_tile = sizes
    send_types = (BF16,) * (STEPS - 1) + (F32,)

    def on_device(green, log_strength, observed, owner_map):
        points, stations = green.shape
        ns = stations // 2
        width = ns // NB
        flat = width * width
        per_lane = LANES // width
        slots = owner_map.shape[0] // n_wide
        units = len(upper_blocks(ns // LANES)) * per_lane
        per = piece_units(sizes, units)
        narrow_units = n_wide * per
        tile_units = n_narrow * narrow_units
        all_units = n_tile * tile_units
        per_pass = n_tile + n_narrow + n_wide - 3

        def buf(lead, kind):
            return pltpu.VMEM((*lead, width, LANES), kind)

        vmem, smem = pl.BlockSpec(memory_space=pltpu.VMEM), pl.BlockSpec(memory_space=pltpu.SMEM)
        unit_table, lane_table = slot_table(NB, width)
        sems = pltpu.SemaphoreType.DMA
        new_log, residual = pl.pallas_call(
            functools.partial(kernel, sizes),
            out_shape=(
                jax.ShapeDtypeStruct((1, points), F32),
                jax.ShapeDtypeStruct((slots, 2 * flat), F32),
            ),
            in_specs=[vmem] * 3 + [smem] * 3,
            out_specs=(vmem, vmem),
            scratch_shapes=[
                pltpu.VMEM((stations, points), BF16),
                pltpu.VMEM((stations, points), BF16),
                buf((2, all_units), F32),
                tuple(None if k == F32 else buf((2, all_units), k) for k in send_types),
                buf((2, tile_units), F32),
                tuple(None if k == F32 else buf((2, tile_units), k) for k in send_types),
                buf((2, narrow_units), F32),
                tuple(None if k == F32 else buf((2, narrow_units), k) for k in send_types),
                buf((2, per), F32),
                pltpu.VMEM((2, ns, ns), BF16),
                buf((STEPS, 2, all_units), BF16),
                buf((2, all_units), BF16),
                pltpu.VMEM((slots, width, 2 * LANES), BF16),
                pltpu.VMEM((slots, width, 2 * LANES), BF16),
                tuple(buf((2, n_tile - 1, tile_units), k) for k in send_types),
                tuple(buf((2, n_narrow - 1, narrow_units), k) for k in send_types),
                tuple(buf((2, n_wide - 1, per), k) for k in send_types),
                sems((2 * STEPS * per_pass,)),
                sems((2 * STEPS * per_pass,)),
                sems((2 * (STEPS + 1) * per_pass,)),
                sems((2 * (STEPS + 1) * per_pass,)),
            ],
            compiler_params=pltpu.CompilerParams(
                collective_id=0, has_side_effects=True, vmem_limit_bytes=60 * 1024 * 1024
            ),
        )(green, log_strength[None, :], observed, owner_map, jnp.asarray(unit_table), jnp.asarray(lane_table))
        return new_log[0], residual

    parts = ("grp", "wide", "narrow", "tile")
    return jax.shard_map(
        on_device, mesh=mesh, in_specs=(P(parts, None), P(parts), P("grp", None), P("grp")),
        out_specs=(P(parts), P(("grp", "wide"), None)), check_vma=False,
    )
```
